256 devices in a mesh: row: 8 (over y, core), col: 32 (over x, z).
Axes of the slice: x: 4, y: 4, z: 8, core: 2. Of those that a mesh axis runs over, the one named last changes fastest.
Arguments:
- tokens: bfloat16 [256, 16384], P('row', 'col'), may hold values from -6 to 6
- out_grad: bfloat16 [256, 16384], P('row', 'col'), may hold values from -6 to 6
- gate_values: bfloat16 [8, 32, 56, 128, 128], P('row', 'col'), may hold values from -0.109375 to 0.109375
- gate_exps: int32 [8, 32, 56], P('row', 'col'), may hold values from -1 to 1
- up_values: bfloat16 [8, 32, 56, 128, 128], P('row', 'col'), may hold values from -0.109375 to 0.109375
- up_exps: int32 [8, 32, 56], P('row', 'col'), may hold values from -1 to 1
- gate_up_ids: int32 [8, 32, 56], P('row', 'col'), may hold values from 0 to 112, as said below
- down_values: bfloat16 [8, 32, 56, 128, 128], P('row', 'col'), may hold values from -0.09375 to 0.09375
- down_exps: int32 [8, 32, 56], P('row', 'col'), may hold values from -1 to 1
- down_ids: int32 [8, 32, 56], P('row', 'col'), may hold values from 0 to 112, as said below
Outputs:
- output: bfloat16 [256, 16384], P('row', 'col')
- input_grad: bfloat16 [256, 16384], P('row', 'col')
- gate_grad: bfloat16 [8, 32, 56, 128, 128], P('row', 'col')
- up_grad: bfloat16 [8, 32, 56, 128, 128], P('row', 'col')
- down_grad: bfloat16 [8, 32, 56, 128, 128], P('row', 'col')
The draws below stay inside these ranges and needn't reach their ends.
Inputs may be any that keep to these rules, and one draw needn't show every extreme that they name: `gate_up_ids`: for each device (first two indices) the live entries name distinct blocks below 112 and come first; the value 112 marks an empty slot; on some device all 56 slots are live. `down_ids`: as for gate_up_ids.
All inputs are finite; a program needn't handle non-finite values.
Results may differ from the reference program's by a relative error of at most 0.005.
Values may be sent and summed in bfloat16 or wider, within the bound.
No kernel may reach another device: no remote copies, remote signals or barrier semaphores. Data moves between devices by JAX's collectives and lax.ppermute only.
A program may use at most 128 MiB of HBM per device.

```python
import jax
import jax.numpy as jnp
from jax import lax

D = 16384
FF_WIN = 28672
BLK = 128
SLOTS = 56
TOKENS = 256
LB = 112
N_ROW = 8
N_COL = 32


def block_list(key):
    count_key, busy_key, score_key = jax.random.split(key, 3)
    devices_all = N_ROW * N_COL
    counts = jax.random.randint(count_key, (devices_all,), SLOTS // 6, SLOTS // 2 + 1)
    busiest = jax.random.randint(busy_key, (), 0, devices_all)
    counts = jnp.where(jnp.arange(devices_all) == busiest, SLOTS, counts)
    scores = jax.random.randint(score_key, (devices_all, LB), 0, 1 << 20) * LB + jnp.arange(LB)[None, :]
    ordering = jnp.argsort(scores, axis=1, stable=True)[:, :SLOTS]
    live_slot = jnp.arange(SLOTS)[None, :] < counts[:, None]
    chosen = jnp.where(live_slot, ordering, LB)
    return chosen.reshape(N_ROW, N_COL, SLOTS).astype(jnp.int32)


def draw_gate_up_ids(key, part):
    return block_list(jax.random.fold_in(key, 11))


def draw_down_ids(key, part):
    return block_list(jax.random.fold_in(key, 23))


def plant(result, rng, least, high):
    longest = result.shape.index(max(result.shape))
    spots = []
    for shift in (0, 1):
        where = [jax.random.randint(jax.random.fold_in(rng, axis), (), 0, length) for axis, length in enumerate(result.shape)]
        where[longest] = (where[longest] + shift) % result.shape[longest]
        spots.append(tuple(where))
    return result.at[spots[0]].set(least).at[spots[1]].set(high)


def steps_of(rng, shape, cuts, low, top_value):
    level, own = 1.0, jax.random.fold_in(rng, 6)
    for axis_at, shards_of in cuts:
        steps = jnp.exp(jax.random.uniform(jax.random.fold_in(own, axis_at), (shards_of,), jnp.float32, low / len(cuts), top_value / len(cuts)))
        level = level * jnp.repeat(steps, shape[axis_at] // shards_of).reshape([-1 if axis == axis_at else 1 for axis in range(len(shape))])
    return level


def bell_draw(stream_key, dims, scale, limit, cuts=(), held_as=jnp.bfloat16):
    entries = scale * jax.random.normal(stream_key, dims, jnp.float32)
    if cuts:
        entries = entries * steps_of(stream_key, dims, cuts, -0.22, 0.18)
    return jnp.clip(entries, -limit, limit).astype(held_as)


def setup_inputs(seed: int = 0) -> dict:
    key_list = jax.random.split(jax.random.key(seed), 11)
    tokens = bell_draw(key_list[0], (TOKENS, D), 1.0, 6.0, ((0, 8), (1, 32)))
    out_grad = bell_draw(key_list[1], (TOKENS, D), 1.0, 6.0, ((0, 8), (1, 32)))
    gate_values = bell_draw(key_list[2], (N_ROW, N_COL, SLOTS, BLK, BLK), (D * SLOTS // (3 * LB)) ** -0.5, 0.109375, ((0, 8), (1, 32)))
    gate_exps = plant(jax.random.randint(key_list[3], (N_ROW, N_COL, SLOTS), -1, 2), jax.random.fold_in(key_list[3], 1), -1, 1).astype(jnp.int32)
    up_values = bell_draw(key_list[4], (N_ROW, N_COL, SLOTS, BLK, BLK), (D * SLOTS // (3 * LB)) ** -0.5, 0.109375, ((0, 8), (1, 32)))
    up_exps = plant(jax.random.randint(key_list[5], (N_ROW, N_COL, SLOTS), -1, 2), jax.random.fold_in(key_list[5], 1), -1, 1).astype(jnp.int32)
    gate_up_ids = draw_gate_up_ids(jax.random.fold_in(key_list[10], 71), 0)
    down_values = bell_draw(key_list[7], (N_ROW, N_COL, SLOTS, BLK, BLK), (FF_WIN * SLOTS // (3 * LB)) ** -0.5, 0.09375, ((0, 8), (1, 32)))
    down_exps = plant(jax.random.randint(key_list[8], (N_ROW, N_COL, SLOTS), -1, 2), jax.random.fold_in(key_list[8], 1), -1, 1).astype(jnp.int32)
    down_ids = draw_down_ids(jax.random.fold_in(key_list[10], 71), 0)
    return dict(tokens=tokens, out_grad=out_grad, gate_values=gate_values, gate_exps=gate_exps, up_values=up_values, up_exps=up_exps, gate_up_ids=gate_up_ids, down_values=down_values, down_exps=down_exps, down_ids=down_ids)


def exponent_scale(exponents):
    return jnp.where(exponents < 0, 0.5, jnp.where(exponents > 0, 2.0, 1.0)).astype(jnp.float32)


def place_column(values, exponents, block_ids, column):
    slot_values = values[:, column]
    slot_scales = exponent_scale(exponents[:, column])
    slot_ids = block_ids[:, column]
    scaled = (slot_values.astype(jnp.float32) * slot_scales[:, :, None, None]).astype(jnp.bfloat16)
    blank = jnp.zeros((LB + 1, BLK, BLK), jnp.bfloat16)

    def one_device(device_values, device_ids):
        return blank.at[device_ids].set(device_values)[:LB]

    return jax.vmap(one_device)(scaled, slot_ids)


def gate_like(values, exponents, block_ids, column):
    placed = place_column(values, exponents, block_ids, column)
    out_blocks = FF_WIN // (N_ROW * BLK)
    in_blocks = D // (N_COL * BLK)
    shaped = placed.reshape(N_ROW, out_blocks, in_blocks, BLK, BLK)
    return shaped.transpose(0, 1, 3, 2, 4).reshape(FF_WIN, D // N_COL)


def down_like(values, exponents, block_ids, column):
    placed = place_column(values, exponents, block_ids, column)
    out_blocks = D // (N_COL * BLK)
    in_blocks = FF_WIN // (N_ROW * BLK)
    shaped = placed.reshape(N_ROW, out_blocks, in_blocks, BLK, BLK)
    return shaped.transpose(1, 3, 0, 2, 4).reshape(D // N_COL, FF_WIN)


def pick_slots(dense_grad, block_ids, exponents, column, order):
    extended = jnp.concatenate([dense_grad, jnp.zeros((N_ROW, 1, BLK, BLK), dense_grad.dtype)], axis=1)
    slot_ids = block_ids[:, column].astype(jnp.int32)
    picked = jnp.take_along_axis(extended, slot_ids[:, :, None, None], axis=1)
    scales = exponent_scale(exponents[:, column])
    return (picked * scales[:, :, None, None]).astype(jnp.bfloat16)


def reference(tokens, out_grad, gate_values, gate_exps, up_values, up_exps, gate_up_ids, down_values, down_exps, down_ids):
    width = D // N_COL
    token_count = tokens.shape[0]
    columns = jnp.arange(N_COL, dtype=jnp.int32)

    def column_slice(array, column):
        return lax.dynamic_slice_in_dim(array, column * width, width, 1)

    def add_forward(carry, column):
        gate_acc, up_acc = carry
        token_cols = column_slice(tokens, column)
        gate_mat = gate_like(gate_values, gate_exps, gate_up_ids, column)
        up_mat = gate_like(up_values, up_exps, gate_up_ids, column)
        gate_part = jnp.dot(token_cols, gate_mat.T, preferred_element_type=jnp.float32)
        up_part = jnp.dot(token_cols, up_mat.T, preferred_element_type=jnp.float32)
        return (gate_acc + gate_part, up_acc + up_part), None

    zeros_hidden = jnp.zeros((token_count, FF_WIN), jnp.float32)
    (gate_sum, up_sum), _ = lax.scan(add_forward, (zeros_hidden, zeros_hidden), columns)
    hidden = (jax.nn.silu(gate_sum) * up_sum).astype(jnp.bfloat16)

    def output_column(column):
        down_mat = down_like(down_values, down_exps, down_ids, column)
        return jnp.dot(hidden, down_mat.T, preferred_element_type=jnp.float32).astype(jnp.bfloat16)

    output = lax.map(output_column, columns).transpose(1, 0, 2).reshape(token_count, D)

    def add_backward(carry, column):
        down_mat = down_like(down_values, down_exps, down_ids, column)
        grad_cols = column_slice(out_grad, column)
        partial_grad = jnp.dot(grad_cols, down_mat, preferred_element_type=jnp.float32)
        return carry + partial_grad, None

    hidden_grad, _ = lax.scan(add_backward, zeros_hidden, columns)
    sigmoid_gate = jax.nn.sigmoid(gate_sum)
    gate_act_grad = (hidden_grad * up_sum * sigmoid_gate * (1.0 + gate_sum * (1.0 - sigmoid_gate))).astype(jnp.bfloat16)
    up_act_grad = (hidden_grad * jax.nn.silu(gate_sum)).astype(jnp.bfloat16)

    def input_column(column):
        gate_mat = gate_like(gate_values, gate_exps, gate_up_ids, column)
        up_mat = gate_like(up_values, up_exps, gate_up_ids, column)
        summed = jnp.dot(gate_act_grad, gate_mat, preferred_element_type=jnp.float32)
        summed = summed + jnp.dot(up_act_grad, up_mat, preferred_element_type=jnp.float32)
        return summed.astype(jnp.bfloat16)

    input_grad = lax.map(input_column, columns).transpose(1, 0, 2).reshape(token_count, D)
    out_blocks = FF_WIN // (N_ROW * BLK)
    in_blocks = width // BLK

    def gate_up_column(column):
        token_cols = column_slice(tokens, column)
        gate_dense = jnp.dot(gate_act_grad.T, token_cols, preferred_element_type=jnp.float32)
        up_dense = jnp.dot(up_act_grad.T, token_cols, preferred_element_type=jnp.float32)

        def to_blocks(dense):
            shaped = dense.reshape(N_ROW, out_blocks, BLK, in_blocks, BLK).transpose(0, 1, 3, 2, 4)
            return shaped.reshape(N_ROW, LB, BLK, BLK)

        return (pick_slots(to_blocks(gate_dense), gate_up_ids, gate_exps, column, 0),
                pick_slots(to_blocks(up_dense), gate_up_ids, up_exps, column, 0))

    gate_stack, up_stack = lax.map(gate_up_column, columns)

    def down_column(column):
        grad_cols = column_slice(out_grad, column)
        dense = jnp.dot(grad_cols.T, hidden, preferred_element_type=jnp.float32)
        shaped = dense.reshape(in_blocks, BLK, N_ROW, out_blocks, BLK).transpose(2, 0, 3, 1, 4)
        return pick_slots(shaped.reshape(N_ROW, LB, BLK, BLK), down_ids, down_exps, column, 1)

    down_stack = lax.map(down_column, columns)
    gate_grad = gate_stack.transpose(1, 0, 2, 3, 4)
    up_grad = up_stack.transpose(1, 0, 2, 3, 4)
    down_grad = down_stack.transpose(1, 0, 2, 3, 4)
    return output, input_grad, gate_grad, up_grad, down_grad
```

```python
import functools

import jax
import jax.numpy as jnp
from jax import lax
from jax.experimental import pallas as pl
from jax.experimental.pallas import tpu as pltpu
from jax.sharding import Mesh
from jax.sharding import PartitionSpec as P

FF_WIN = 28672
BLK = 128
F32, BF16 = jnp.float32, jnp.bfloat16
VMEM_LIMIT = 56 << 20
UP_CUT = 10 * BLK


def slot_scale(exponent):
    return jnp.where(exponent < 0, 0.5, jnp.where(exponent > 0, 2.0, 1.0)).astype(F32)


def place_body(in_blocks, block_count, ids, exps, values, dense):
    dense[...] = jnp.zeros_like(dense)

    def place(s, carry):
        block = ids[s]

        @pl.when(block < block_count)
        def _():
            row = pl.multiple_of(lax.div(block, in_blocks) * BLK, BLK)
            col = pl.multiple_of(lax.rem(block, in_blocks) * BLK, BLK)
            scaled = values[s].astype(F32) * slot_scale(exps[s])
            dense[pl.ds(row, BLK), pl.ds(col, BLK)] = scaled.astype(BF16)

        return carry

    lax.fori_loop(0, values.shape[0], place, 0)


def dense_matrix(values, exps, ids, out_blocks, in_blocks):
    return pl.pallas_call(
        functools.partial(place_body, in_blocks, out_blocks * in_blocks),
        out_shape=jax.ShapeDtypeStruct((out_blocks * BLK, in_blocks * BLK), BF16),
        in_specs=[
            pl.BlockSpec(memory_space=pltpu.SMEM),
            pl.BlockSpec(memory_space=pltpu.SMEM),
            pl.BlockSpec(memory_space=pltpu.VMEM),
        ],
        out_specs=pl.BlockSpec(memory_space=pltpu.VMEM),
        compiler_params=pltpu.CompilerParams(vmem_limit_bytes=VMEM_LIMIT),
    )(ids, exps, values)


def fill_dense(dense, column, out_acts, in_acts):
    wide = 2 * BLK
    for c in range(out_acts.shape[1] // wide):
        dense[column + c * wide : column + (c + 1) * wide, :] = lax.dot_general(
            out_acts[:, c * wide : (c + 1) * wide],
            in_acts[...],
            (((0,), (0,)), ((), ())),
            preferred_element_type=F32,
        )


def pick_slots(in_blocks, block_count, ids, exps, dense, grads):
    def pick(s, carry):
        block = ids[s]
        live = block < block_count

        @pl.when(live)
        def _():
            row = pl.multiple_of(lax.div(block, in_blocks) * BLK, BLK)
            col = pl.multiple_of(lax.rem(block, in_blocks) * BLK, BLK)
            picked = dense[pl.ds(row, BLK), pl.ds(col, BLK)] * slot_scale(exps[s])
            grads[s] = picked.astype(BF16)

        @pl.when(jnp.logical_not(live))
        def _():
            grads[s] = jnp.zeros((BLK, BLK), BF16)

        return carry

    lax.fori_loop(0, grads.shape[0], pick, 0)


def pair_grad_body(in_blocks, ids, gate_e, up_e, left, right, tokens, gate_g, up_g, dense):
    hidden = dense.shape[0]
    count = hidden // BLK * in_blocks
    fill_dense(dense, 0, left.at[:, :hidden], tokens)
    pick_slots(in_blocks, count, ids, gate_e, dense, gate_g)
    fill_dense(dense, 0, left.at[:, hidden:], tokens)
    fill_dense(dense, left.shape[1] - hidden, right, tokens)
    pick_slots(in_blocks, count, ids, up_e, dense, up_g)


def low_grad_body(in_blocks, ids, exps, out_acts, in_acts, grads, dense):
    flipped = out_acts[...].T
    wide = 2 * BLK
    for c in range(in_blocks * BLK // wide):
        cols = slice(c * wide, (c + 1) * wide)
        dense[:, cols] = jnp.dot(flipped, in_acts[:, cols], preferred_element_type=F32)
    pick_slots(in_blocks, dense.shape[0] // BLK * in_blocks, ids, exps, dense, grads)


def grad_call(body, scalars, arrays, outs, dense_shape):
    slots = scalars[0].shape[0]
    smem, vmem = (pl.BlockSpec(memory_space=m) for m in (pltpu.SMEM, pltpu.VMEM))
    return pl.pallas_call(
        body,
        out_shape=[jax.ShapeDtypeStruct((slots, BLK, BLK), BF16)] * outs,
        in_specs=[smem] * len(scalars) + [vmem] * len(arrays),
        out_specs=[vmem] * outs,
        scratch_shapes=[pltpu.VMEM(dense_shape, F32)],
        compiler_params=pltpu.CompilerParams(vmem_limit_bytes=VMEM_LIMIT),
    )(*scalars, *arrays)


def dot_nt(a, b, kind):
    return lax.dot_general(
        a, b, (((1,), (1,)), ((), ())), preferred_element_type=F32
    ).astype(kind)


def dot_nn(a, b, kind):
    return jnp.dot(a, b, preferred_element_type=F32).astype(kind)


def exchange_sum(part, axis):
    size = lax.axis_size(axis)
    got = lax.all_to_all(part, axis, split_axis=0, concat_axis=0, tiled=True)
    return jnp.sum(got.reshape(size, -1, part.shape[1]).astype(F32), axis=0)


def spread(rows, axis):
    size = lax.axis_size(axis)
    copies = jnp.broadcast_to(rows[None], (size, *rows.shape))
    copies = copies.reshape(size * rows.shape[0], rows.shape[1])
    return lax.all_to_all(copies, axis, split_axis=0, concat_axis=0, tiled=True)


def shift(rows, axis, step):
    size = lax.axis_size(axis)
    return lax.ppermute(rows, axis, [(i, (i + step) % size) for i in range(size)])


def turn(rows, steps):
    return jnp.roll(rows, steps * (rows.shape[0] // 4), axis=0)


def reduce_x(part):
    rows = part.shape[0] // 4
    total = part[:rows].astype(F32)
    for k in range(1, 4):
        total = total + shift(part[k * rows : (k + 1) * rows], "x", k).astype(F32)
    return total


def gather_x(rows):
    return jnp.concatenate([rows] + [shift(rows, "x", -k) for k in range(1, 4)], axis=0)


def on_device(
    tokens,
    out_grad,
    gate_values,
    gate_exps,
    up_values,
    up_exps,
    gate_up_ids,
    down_values,
    down_exps,
    down_ids,
):
    width = tokens.shape[1]
    width_blocks = width // BLK
    hidden = FF_WIN // (lax.axis_size("y") * lax.axis_size("core"))
    hidden_blocks = hidden // BLK
    pair_ids, low_ids = gate_up_ids[0, 0], down_ids[0, 0]
    gate_e, up_e, down_e = gate_exps[0, 0], up_exps[0, 0], down_exps[0, 0]

    both = spread(jnp.concatenate([tokens, out_grad], axis=1), ("y", "core"))
    place = lax.axis_index("x")
    both = turn(both, -place)
    tokens_all, grads_all = both[:, :width], both[:, width:]

    gate_w = dense_matrix(gate_values[0, 0], gate_e, pair_ids, hidden_blocks, width_blocks)
    up_w = dense_matrix(up_values[0, 0], up_e, pair_ids, hidden_blocks, width_blocks)
    down_w = dense_matrix(down_values[0, 0], down_e, low_ids, width_blocks, hidden_blocks)

    gate_x = reduce_x(dot_nt(tokens_all, gate_w, BF16))
    up_x = reduce_x(dot_nt(tokens_all, up_w, BF16))
    back_x = reduce_x(dot_nn(grads_all, down_w, BF16))
    gate_sum = exchange_sum(gate_x, "z")
    up_sum = exchange_sum(up_x, "z")
    back_sum = exchange_sum(back_x, "z")

    sigmoid = jax.nn.sigmoid(gate_sum)
    silu = gate_sum * sigmoid
    act = (silu * up_sum).astype(BF16)
    gate_piece = back_sum * up_sum * sigmoid * (1.0 + gate_sum * (1.0 - sigmoid))
    gate_piece, up_piece = gate_piece.astype(BF16), (back_sum * silu).astype(BF16)

    act_all = gather_x(spread(act, "z"))
    left = jnp.concatenate([gate_piece, up_piece[:, :UP_CUT]], axis=1)
    left = gather_x(spread(left, "z"))
    right = spread(gather_x(up_piece[:, UP_CUT:]), "z")
    right = right.reshape(8, 4, -1, right.shape[1]).transpose(1, 0, 2, 3)
    right = right.reshape(left.shape[0], -1)

    output_part = dot_nt(act_all, down_w, F32)
    input_part = dot_nn(left[:, :hidden], gate_w, F32)
    input_part = input_part + dot_nn(left[:, hidden:], up_w[:UP_CUT], F32)
    input_part = input_part + dot_nn(right, up_w[UP_CUT:], F32)
    output_rows = exchange_sum(turn(output_part, place), ("y", "core")).astype(BF16)
    input_rows = exchange_sum(turn(input_part, place), ("y", "core")).astype(BF16)

    [down_grad] = grad_call(
        functools.partial(low_grad_body, hidden_blocks),
        (low_ids, down_e),
        (grads_all, act_all),
        1,
        (width, hidden),
    )
    gate_grad, up_grad = grad_call(
        functools.partial(pair_grad_body, width_blocks),
        (pair_ids, gate_e, up_e),
        (left, right, tokens_all),
        2,
        (hidden, width),
    )
    grads = (g[None, None] for g in (gate_grad, up_grad, down_grad))
    return output_rows, input_rows, *grads


def solution(mesh):
    shape = (4, 2, 4, 8)
    split = Mesh(mesh.devices.reshape(shape), ("y", "core", "x", "z"))
    row, col = ("y", "core"), ("x", "z")
    blocks, slots = P(row, col, None, None, None), P(row, col, None)
    return jax.shard_map(
        on_device,
        mesh=split,
        in_specs=(
            P(row, col),
            P(row, col),
            blocks,
            slots,
            blocks,
            slots,
            slots,
            blocks,
            slots,
            slots,
        ),
        out_specs=(P(row, col), P(row, col), blocks, blocks, blocks),
        check_vma=False,
    )
```

```python
import functools

import jax
import jax.numpy as jnp
from jax import lax
from jax.experimental import pallas as pl
from jax.experimental.pallas import tpu as pltpu
from jax.sharding import Mesh
from jax.sharding import PartitionSpec as P

FF_WIN = 28672
BLK = 128
F32, BF16 = jnp.float32, jnp.bfloat16
VMEM_LIMIT = 56 << 20


def slot_scale(exponent):
    return jnp.where(exponent < 0, 0.5, jnp.where(exponent > 0, 2.0, 1.0)).astype(F32)


def place_body(in_blocks, block_count, ids, exps, values, dense):
    dense[...] = jnp.zeros_like(dense)

    def place(s, carry):
        block = ids[s]

        @pl.when(block < block_count)
        def _():
            row = pl.multiple_of(lax.div(block, in_blocks) * BLK, BLK)
            col = pl.multiple_of(lax.rem(block, in_blocks) * BLK, BLK)
            scaled = values[s].astype(F32) * slot_scale(exps[s])
            dense[pl.ds(row, BLK), pl.ds(col, BLK)] = scaled.astype(BF16)

        return carry

    lax.fori_loop(0, values.shape[0], place, 0)


def dense_matrix(values, exps, ids, out_blocks, in_blocks):
    return pl.pallas_call(
        functools.partial(place_body, in_blocks, out_blocks * in_blocks),
        out_shape=jax.ShapeDtypeStruct((out_blocks * BLK, in_blocks * BLK), BF16),
        in_specs=[
            pl.BlockSpec(memory_space=pltpu.SMEM),
            pl.BlockSpec(memory_space=pltpu.SMEM),
            pl.BlockSpec(memory_space=pltpu.VMEM),
        ],
        out_specs=pl.BlockSpec(memory_space=pltpu.VMEM),
        compiler_params=pltpu.CompilerParams(vmem_limit_bytes=VMEM_LIMIT),
    )(ids, exps, values)


def fill_dense(dense, column, out_acts, in_acts):
    wide = 2 * BLK
    for c in range(out_acts.shape[1] // wide):
        dense[column + c * wide : column + (c + 1) * wide, :] = lax.dot_general(
            out_acts[:, c * wide : (c + 1) * wide],
            in_acts[...],
            (((0,), (0,)), ((), ())),
            preferred_element_type=F32,
        )


def pick_slots(in_blocks, block_count, ids, exps, dense, grads):
    def pick(s, carry):
        block = ids[s]
        live = block < block_count

        @pl.when(live)
        def _():
            row = pl.multiple_of(lax.div(block, in_blocks) * BLK, BLK)
            col = pl.multiple_of(lax.rem(block, in_blocks) * BLK, BLK)
            picked = dense[pl.ds(row, BLK), pl.ds(col, BLK)] * slot_scale(exps[s])
            grads[s] = picked.astype(BF16)

        @pl.when(jnp.logical_not(live))
        def _():
            grads[s] = jnp.zeros((BLK, BLK), BF16)

        return carry

    lax.fori_loop(0, grads.shape[0], pick, 0)


def gather_parts(whole, parts):
    rows = whole.shape[0] // len(parts)
    for k, part in enumerate(parts):
        whole[k * rows : (k + 1) * rows, :] = part[...]


def turned_body(place, first, matrix, *rest):
    *parts, result, whole = rest
    gather_parts(whole, parts)
    total = first[...] + jnp.dot(whole[...], matrix[...], preferred_element_type=F32)
    rows = total.shape[0] // 4
    for k in range(4):
        at = pl.multiple_of(lax.rem(place[0] + k, 4) * rows, rows)
        result[pl.ds(at, rows), :] = total[k * rows : (k + 1) * rows]


def turned_sum(place, first, matrix, parts):
    smem, vmem = (pl.BlockSpec(memory_space=m) for m in (pltpu.SMEM, pltpu.VMEM))
    return pl.pallas_call(
        turned_body,
        out_shape=jax.ShapeDtypeStruct(first.shape, F32),
        in_specs=[smem] + [vmem] * (2 + len(parts)),
        out_specs=vmem,
        scratch_shapes=[pltpu.VMEM((first.shape[0], matrix.shape[0]), BF16)],
        compiler_params=pltpu.CompilerParams(vmem_limit_bytes=VMEM_LIMIT),
    )(place[None].astype(jnp.int32), first, matrix, *parts)


def gate_body(in_blocks, ids, exps, tokens, matrix, *rest):
    *parts, onward, grads, whole, dense = rest
    gather_parts(whole, parts)
    onward[...] = jnp.dot(whole[...], matrix[...], preferred_element_type=F32)
    fill_dense(dense, 0, whole, tokens)
    pick_slots(in_blocks, dense.shape[0] // BLK * in_blocks, ids, exps, dense, grads)


def low_body(in_blocks, ids, exps, out_acts, matrix, *rest):
    *parts, onward, grads, whole, dense = rest
    gather_parts(whole, parts)
    onward[...] = lax.dot_general(
        whole[...], matrix[...], (((1,), (1,)), ((), ())), preferred_element_type=F32
    )
    flipped = out_acts[...].T
    wide = 2 * BLK
    for c in range(in_blocks * BLK // wide):
        cols = slice(c * wide, (c + 1) * wide)
        dense[:, cols] = jnp.dot(flipped, whole[:, cols], preferred_element_type=F32)
    pick_slots(in_blocks, dense.shape[0] // BLK * in_blocks, ids, exps, dense, grads)


def onward_and_grad(body, in_blocks, ids, exps, acts, matrix, parts):
    slots, columns = ids.shape[0], parts[0].shape[1]
    smem, vmem = (pl.BlockSpec(memory_space=m) for m in (pltpu.SMEM, pltpu.VMEM))
    onward, grads = pl.pallas_call(
        functools.partial(body, in_blocks),
        out_shape=[
            jax.ShapeDtypeStruct(acts.shape, F32),
            jax.ShapeDtypeStruct((slots, BLK, BLK), BF16),
        ],
        in_specs=[smem] * 2 + [vmem] * (2 + len(parts)),
        out_specs=[vmem] * 2,
        scratch_shapes=[
            pltpu.VMEM((acts.shape[0], columns), BF16),
            pltpu.VMEM(matrix.shape, F32),
        ],
        compiler_params=pltpu.CompilerParams(vmem_limit_bytes=VMEM_LIMIT),
    )(ids, exps, acts, matrix, *parts)
    return onward, grads


def up_body(in_blocks, ids, exps, tokens, *rest):
    *parts, grads, whole, dense = rest
    gather_parts(whole, parts)
    fill_dense(dense, 0, whole, tokens)
    pick_slots(in_blocks, dense.shape[0] // BLK * in_blocks, ids, exps, dense, grads)


def up_gradient(in_blocks, ids, exps, tokens, parts):
    slots, columns = ids.shape[0], parts[0].shape[1]
    smem, vmem = (pl.BlockSpec(memory_space=m) for m in (pltpu.SMEM, pltpu.VMEM))
    return pl.pallas_call(
        functools.partial(up_body, in_blocks),
        out_shape=jax.ShapeDtypeStruct((slots, BLK, BLK), BF16),
        in_specs=[smem] * 2 + [vmem] * (1 + len(parts)),
        out_specs=vmem,
        scratch_shapes=[
            pltpu.VMEM((tokens.shape[0], columns), BF16),
            pltpu.VMEM((columns, tokens.shape[1]), F32),
        ],
        compiler_params=pltpu.CompilerParams(vmem_limit_bytes=VMEM_LIMIT),
    )(ids, exps, tokens, *parts)


def onward_and_grad(body, in_blocks, ids, exps, acts, matrix, parts):
    slots, columns = ids.shape[0], parts[0].shape[1]
    smem, vmem = (pl.BlockSpec(memory_space=m) for m in (pltpu.SMEM, pltpu.VMEM))
    return pl.pallas_call(
        functools.partial(body, in_blocks),
        out_shape=[
            jax.ShapeDtypeStruct(acts.shape, F32),
            jax.ShapeDtypeStruct((slots, BLK, BLK), BF16),
        ],
        in_specs=[smem] * 2 + [vmem] * (2 + len(parts)),
        out_specs=[vmem] * 2,
        scratch_shapes=[
            pltpu.VMEM((acts.shape[0], columns), BF16),
            pltpu.VMEM(matrix.shape, F32),
        ],
        compiler_params=pltpu.CompilerParams(vmem_limit_bytes=VMEM_LIMIT),
    )(ids, exps, acts, matrix, *parts)


def part_body(flipped, acts, matrix, own, *sent):
    wide = 2 * BLK
    rows = own.shape[0]
    for c in range(own.shape[1] // wide):
        cols = slice(c * wide, (c + 1) * wide)
        if flipped:
            part = lax.dot_general(
                acts[...], matrix[cols, :], (((1,), (1,)), ((), ())), preferred_element_type=F32
            )
        else:
            part = jnp.dot(acts[...], matrix[:, cols], preferred_element_type=F32)
        own[:, cols] = part[:rows]
        for k, chunk in enumerate(sent):
            chunk[:, cols] = part[(k + 1) * rows : (k + 2) * rows].astype(BF16)


def part_chunks(acts, matrix, flipped):
    rows, columns = acts.shape[0] // 4, matrix.shape[0 if flipped else 1]
    vmem = pl.BlockSpec(memory_space=pltpu.VMEM)
    return pl.pallas_call(
        functools.partial(part_body, flipped),
        out_shape=[jax.ShapeDtypeStruct((rows, columns), F32)]
        + [jax.ShapeDtypeStruct((rows, columns), BF16)] * 3,
        in_specs=[vmem] * 2,
        out_specs=[vmem] * 4,
        compiler_params=pltpu.CompilerParams(vmem_limit_bytes=VMEM_LIMIT),
    )(acts, matrix)


def dot_nt(a, b, kind):
    return lax.dot_general(
        a, b, (((1,), (1,)), ((), ())), preferred_element_type=F32
    ).astype(kind)


def dot_nn(a, b, kind):
    return jnp.dot(a, b, preferred_element_type=F32).astype(kind)


def exchange_sum(part, axis):
    size = lax.axis_size(axis)
    got = lax.all_to_all(part, axis, split_axis=0, concat_axis=0, tiled=True)
    return jnp.sum(got.reshape(size, -1, part.shape[1]).astype(F32), axis=0)


def spread(rows, axis):
    size = lax.axis_size(axis)
    copies = jnp.broadcast_to(rows[None], (size, *rows.shape))
    copies = copies.reshape(size * rows.shape[0], rows.shape[1])
    return lax.all_to_all(copies, axis, split_axis=0, concat_axis=0, tiled=True)


def shift(rows, axis, step):
    size = lax.axis_size(axis)
    return lax.ppermute(rows, axis, [(i, (i + step) % size) for i in range(size)])


def turn(rows, steps):
    return jnp.roll(rows, steps * (rows.shape[0] // 4), axis=0)


def cross_x(chunks):
    total = chunks[0]
    for k in range(1, 4):
        total = total + shift(chunks[k], "x", k).astype(F32)
    return total


def own_rest(total, place_z):
    rows = total.shape[0] // 8
    own = lax.dynamic_slice_in_dim(total, place_z * rows, rows, axis=0)
    return own - lax.reduce_precision(own, exponent_bits=8, mantissa_bits=7)


def cross_z(total, place_z):
    return exchange_sum(total.astype(BF16), "z") + own_rest(total, place_z)


def after(value, *others):
    return lax.optimization_barrier((value, *others))[0]


def parts_x(rows):
    return [rows] + [shift(rows, "x", -k) for k in range(1, 4)]


def on_device(
    tokens,
    out_grad,
    gate_values,
    gate_exps,
    up_values,
    up_exps,
    gate_up_ids,
    down_values,
    down_exps,
    down_ids,
):
    width = tokens.shape[1]
    width_blocks = width // BLK
    hidden = FF_WIN // (lax.axis_size("y") * lax.axis_size("core"))
    hidden_blocks = hidden // BLK
    pair_ids, low_ids = gate_up_ids[0, 0], down_ids[0, 0]
    gate_e, up_e, down_e = gate_exps[0, 0], up_exps[0, 0], down_exps[0, 0]

    gate_w = dense_matrix(gate_values[0, 0], gate_e, pair_ids, hidden_blocks, width_blocks)
    up_w = dense_matrix(up_values[0, 0], up_e, pair_ids, hidden_blocks, width_blocks)
    both = spread(jnp.concatenate([tokens, out_grad], axis=1), ("y", "core"))
    both, gate_w, up_w = lax.optimization_barrier((both, gate_w, up_w))
    place, place_z = lax.axis_index("x"), lax.axis_index("z")
    both = turn(both, -place)
    tokens_all, grads_all = both[:, :width], both[:, width:]

    gate_chunks = part_chunks(tokens_all, gate_w, True)
    up_chunks = part_chunks(tokens_all, up_w, True)
    down_w = dense_matrix(
        after(down_values, *up_chunks)[0, 0], down_e, low_ids, width_blocks, hidden_blocks
    )
    back_chunks = part_chunks(grads_all, down_w, False)
    gate_x, up_x, back_x = cross_x(gate_chunks), cross_x(up_chunks), cross_x(back_chunks)
    gate_sum = cross_z(after(gate_x, *back_chunks), place_z)
    up_sum = cross_z(up_x, place_z)

    sigmoid = jax.nn.sigmoid(gate_sum)
    silu = gate_sum * sigmoid
    act = (silu * up_sum).astype(BF16)
    slope = up_sum * sigmoid * (1.0 + gate_sum * (1.0 - sigmoid))
    act, slope, silu = lax.optimization_barrier((act, slope, silu))

    carried = jnp.concatenate([back_x.astype(BF16), jnp.tile(act, (8, 1))], axis=1)
    carried = lax.all_to_all(carried, "z", split_axis=0, concat_axis=0, tiled=True)
    back_sum = jnp.sum(carried[:, :hidden].reshape(8, -1, hidden).astype(F32), axis=0)
    back_sum = back_sum + own_rest(back_x, place_z)
    gate_piece, up_piece = (back_sum * slope).astype(BF16), (back_sum * silu).astype(BF16)

    act_parts = parts_x(carried[:, hidden:])
    gate_parts = parts_x(spread(gate_piece, "z"))
    up_parts = parts_x(spread(after(up_piece, act_parts), "z"))

    output_part, down_grad = onward_and_grad(
        low_body,
        hidden_blocks,
        low_ids,
        down_e,
        after(grads_all, gate_parts[1]),
        down_w,
        act_parts,
    )
    output_rows = exchange_sum(turn(output_part, place), ("y", "core")).astype(BF16)
    input_part, gate_grad = onward_and_grad(
        gate_body, width_blocks, pair_ids, gate_e, tokens_all, gate_w, after(gate_parts, down_grad)
    )
    up_parts = after(up_parts, gate_grad)
    input_part = turned_sum(place, input_part, up_w, up_parts)
    input_rows = exchange_sum(input_part, ("y", "core")).astype(BF16)
    up_grad = up_gradient(width_blocks, pair_ids, up_e, tokens_all, up_parts)
    grads = (g[None, None] for g in (gate_grad, up_grad, down_grad))
    return output_rows, input_rows, *grads


def solution(mesh):
    shape = (4, 2, 4, 8)
    split = Mesh(mesh.devices.reshape(shape), ("y", "core", "x", "z"))
    row, col = ("y", "core"), ("x", "z")
    blocks, slots = P(row, col, None, None, None), P(row, col, None)
    return jax.shard_map(
        on_device,
        mesh=split,
        in_specs=(
            P(row, col),
            P(row, col),
            blocks,
            slots,
            blocks,
            slots,
            slots,
            blocks,
            slots,
            slots,
        ),
        out_specs=(P(row, col), P(row, col), blocks, blocks, blocks),
        check_vma=False,
    )
```

```python
import functools

import jax
import jax.numpy as jnp
from jax import lax
from jax.experimental import pallas as pl
from jax.experimental.pallas import tpu as pltpu
from jax.sharding import Mesh
from jax.sharding import PartitionSpec as P

FF_WIN = 28672
BLK = 128
F32, BF16 = jnp.float32, jnp.bfloat16
VMEM_LIMIT = 56 << 20
UP_CUT = 2 * BLK


def slot_scale(exponent):
    return jnp.where(exponent < 0, 0.5, jnp.where(exponent > 0, 2.0, 1.0)).astype(F32)


def place_body(in_blocks, block_count, ids, exps, values, dense):
    dense[...] = jnp.zeros_like(dense)

    def place(s, carry):
        block = ids[s]

        @pl.when(block < block_count)
        def _():
            row = pl.multiple_of(lax.div(block, in_blocks) * BLK, BLK)
            col = pl.multiple_of(lax.rem(block, in_blocks) * BLK, BLK)
            scaled = values[s].astype(F32) * slot_scale(exps[s])
            dense[pl.ds(row, BLK), pl.ds(col, BLK)] = scaled.astype(BF16)

        return carry

    lax.fori_loop(0, values.shape[0], place, 0)


def dense_matrix(values, exps, ids, out_blocks, in_blocks):
    return pl.pallas_call(
        functools.partial(place_body, in_blocks, out_blocks * in_blocks),
        out_shape=jax.ShapeDtypeStruct((out_blocks * BLK, in_blocks * BLK), BF16),
        in_specs=[
            pl.BlockSpec(memory_space=pltpu.SMEM),
            pl.BlockSpec(memory_space=pltpu.SMEM),
            pl.BlockSpec(memory_space=pltpu.VMEM),
        ],
        out_specs=pl.BlockSpec(memory_space=pltpu.VMEM),
        compiler_params=pltpu.CompilerParams(vmem_limit_bytes=VMEM_LIMIT),
    )(ids, exps, values)


def fill_dense(dense, column, out_acts, in_acts):
    wide = 2 * BLK
    for c in range(out_acts.shape[1] // wide):
        dense[column + c * wide : column + (c + 1) * wide, :] = lax.dot_general(
            out_acts[:, c * wide : (c + 1) * wide],
            in_acts[...],
            (((0,), (0,)), ((), ())),
            preferred_element_type=F32,
        )


def pick_slots(in_blocks, block_count, ids, exps, dense, grads):
    def pick(s, carry):
        block = ids[s]
        live = block < block_count

        @pl.when(live)
        def _():
            row = pl.multiple_of(lax.div(block, in_blocks) * BLK, BLK)
            col = pl.multiple_of(lax.rem(block, in_blocks) * BLK, BLK)
            picked = dense[pl.ds(row, BLK), pl.ds(col, BLK)] * slot_scale(exps[s])
            grads[s] = picked.astype(BF16)

        @pl.when(jnp.logical_not(live))
        def _():
            grads[s] = jnp.zeros((BLK, BLK), BF16)

        return carry

    lax.fori_loop(0, grads.shape[0], pick, 0)


def gather_parts(whole, parts):
    rows = whole.shape[0] // len(parts)
    for k, part in enumerate(parts):
        whole[k * rows : (k + 1) * rows, :] = part[...]


def pair_body(in_blocks, ids, gate_e, up_e, tokens, right_tokens, right, *rest):
    *parts, gate_g, up_g, left, dense = rest
    hidden = dense.shape[0]
    count = hidden // BLK * in_blocks
    gather_parts(left, parts)
    fill_dense(dense, 0, left.at[:, :hidden], tokens)
    pick_slots(in_blocks, count, ids, gate_e, dense, gate_g)
    fill_dense(dense, 0, left.at[:, hidden:], tokens)
    fill_dense(dense, left.shape[1] - hidden, right, right_tokens)
    pick_slots(in_blocks, count, ids, up_e, dense, up_g)


def pair_grads(body, scalars, arrays, dense_shape):
    slots = jax.ShapeDtypeStruct((scalars[0].shape[0], BLK, BLK), BF16)
    left = (arrays[0].shape[0], arrays[-1].shape[1])
    smem, vmem = (pl.BlockSpec(memory_space=m) for m in (pltpu.SMEM, pltpu.VMEM))
    return pl.pallas_call(
        body,
        out_shape=[slots] * 2,
        in_specs=[smem] * len(scalars) + [vmem] * len(arrays),
        out_specs=[vmem] * 2,
        scratch_shapes=[pltpu.VMEM(left, BF16), pltpu.VMEM(dense_shape, F32)],
        compiler_params=pltpu.CompilerParams(vmem_limit_bytes=VMEM_LIMIT),
    )(*scalars, *arrays)


def turned_body(place, first, gate_w, up_w, *rest):
    *parts, result, left = rest
    gather_parts(left, parts)
    cut = gate_w.shape[0]
    total = first[...] + jnp.dot(left[:, :cut], gate_w[...], preferred_element_type=F32)
    total = total + jnp.dot(
        left[:, cut:], up_w[...], preferred_element_type=F32
    )
    rows = total.shape[0] // 4
    for k in range(4):
        at = pl.multiple_of(lax.rem(place[0] + k, 4) * rows, rows)
        result[pl.ds(at, rows), :] = total[k * rows : (k + 1) * rows]


def turned_sum(place, first, gate_w, up_w, parts):
    rows, columns = len(parts) * parts[0].shape[0], parts[0].shape[1]
    smem = pl.BlockSpec(memory_space=pltpu.SMEM)

    def whole(array):
        return pl.BlockSpec(array.shape, lambda i: (0, 0))

    some_up = pl.BlockSpec((columns - gate_w.shape[0], up_w.shape[1]), lambda i: (0, 0))
    return pl.pallas_call(
        turned_body,
        grid=(1,),
        out_shape=jax.ShapeDtypeStruct(first.shape, F32),
        in_specs=[smem, whole(first), whole(gate_w), some_up] + [whole(part) for part in parts],
        out_specs=whole(first),
        scratch_shapes=[pltpu.VMEM((rows, columns), BF16)],
        compiler_params=pltpu.CompilerParams(vmem_limit_bytes=VMEM_LIMIT),
    )(place[None].astype(jnp.int32), first, gate_w, up_w, *parts)


def low_body(in_blocks, ids, exps, out_acts, matrix, *rest):
    *parts, onward, grads, whole, dense = rest
    gather_parts(whole, parts)
    onward[...] = lax.dot_general(
        whole[...], matrix[...], (((1,), (1,)), ((), ())), preferred_element_type=F32
    )
    flipped = out_acts[...].T
    wide = 2 * BLK
    for c in range(in_blocks * BLK // wide):
        cols = slice(c * wide, (c + 1) * wide)
        dense[:, cols] = jnp.dot(flipped, whole[:, cols], preferred_element_type=F32)
    pick_slots(in_blocks, dense.shape[0] // BLK * in_blocks, ids, exps, dense, grads)


def onward_and_grad(body, in_blocks, ids, exps, acts, matrix, parts):
    slots, columns = ids.shape[0], parts[0].shape[1]
    smem, vmem = (pl.BlockSpec(memory_space=m) for m in (pltpu.SMEM, pltpu.VMEM))
    onward, grads = pl.pallas_call(
        functools.partial(body, in_blocks),
        out_shape=[
            jax.ShapeDtypeStruct(acts.shape, F32),
            jax.ShapeDtypeStruct((slots, BLK, BLK), BF16),
        ],
        in_specs=[smem] * 2 + [vmem] * (2 + len(parts)),
        out_specs=[vmem] * 2,
        scratch_shapes=[
            pltpu.VMEM((acts.shape[0], columns), BF16),
            pltpu.VMEM(matrix.shape, F32),
        ],
        compiler_params=pltpu.CompilerParams(vmem_limit_bytes=VMEM_LIMIT),
    )(ids, exps, acts, matrix, *parts)
    return onward, grads


def part_body(flipped, acts, matrix, own, *sent):
    wide = 2 * BLK
    rows = own.shape[0]
    for c in range(own.shape[1] // wide):
        cols = slice(c * wide, (c + 1) * wide)
        if flipped:
            part = lax.dot_general(
                acts[...], matrix[cols, :], (((1,), (1,)), ((), ())), preferred_element_type=F32
            )
        else:
            part = jnp.dot(acts[...], matrix[:, cols], preferred_element_type=F32)
        own[:, cols] = part[:rows]
        for k, chunk in enumerate(sent):
            chunk[:, cols] = part[(k + 1) * rows : (k + 2) * rows].astype(BF16)


def part_chunks(acts, matrix, flipped):
    rows, columns = acts.shape[0] // 4, matrix.shape[0 if flipped else 1]
    vmem = pl.BlockSpec(memory_space=pltpu.VMEM)
    return pl.pallas_call(
        functools.partial(part_body, flipped),
        out_shape=[jax.ShapeDtypeStruct((rows, columns), F32)]
        + [jax.ShapeDtypeStruct((rows, columns), BF16)] * 3,
        in_specs=[vmem] * 2,
        out_specs=[vmem] * 4,
        compiler_params=pltpu.CompilerParams(vmem_limit_bytes=VMEM_LIMIT),
    )(acts, matrix)


def dot_nn(a, b, kind):
    return jnp.dot(a, b, preferred_element_type=F32).astype(kind)


def exchange_sum(part, axis):
    size = lax.axis_size(axis)
    got = lax.all_to_all(part, axis, split_axis=0, concat_axis=0, tiled=True)
    return jnp.sum(got.reshape(size, -1, part.shape[1]).astype(F32), axis=0)


def spread(rows, axis):
    size = lax.axis_size(axis)
    copies = jnp.broadcast_to(rows[None], (size, *rows.shape))
    copies = copies.reshape(size * rows.shape[0], rows.shape[1])
    return lax.all_to_all(copies, axis, split_axis=0, concat_axis=0, tiled=True)


def shift(rows, axis, step):
    size = lax.axis_size(axis)
    return lax.ppermute(rows, axis, [(i, (i + step) % size) for i in range(size)])


def turn(rows, steps):
    return jnp.roll(rows, steps * (rows.shape[0] // 4), axis=0)


def cross_x(chunks):
    total = chunks[0]
    for k in range(1, 4):
        total = total + shift(chunks[k], "x", k).astype(F32)
    return total


def own_rest(total, place_z):
    rows = total.shape[0] // 8
    own = lax.dynamic_slice_in_dim(total, place_z * rows, rows, axis=0)
    return own - lax.reduce_precision(own, exponent_bits=8, mantissa_bits=7)


def cross_z(total, place_z):
    return exchange_sum(total.astype(BF16), "z") + own_rest(total, place_z)


def swap_order(rows, outer, inner):
    grouped = rows.reshape(outer, inner, -1, rows.shape[1])
    return grouped.transpose(1, 0, 2, 3).reshape(rows.shape)


def after(value, *others):
    return lax.optimization_barrier((value, *others))[0]


def parts_x(rows):
    return [rows] + [shift(rows, "x", -k) for k in range(1, 4)]


def on_device(
    tokens,
    out_grad,
    gate_values,
    gate_exps,
    up_values,
    up_exps,
    gate_up_ids,
    down_values,
    down_exps,
    down_ids,
):
    width = tokens.shape[1]
    width_blocks = width // BLK
    hidden = FF_WIN // (lax.axis_size("y") * lax.axis_size("core"))
    hidden_blocks = hidden // BLK
    pair_ids, low_ids = gate_up_ids[0, 0], down_ids[0, 0]
    gate_e, up_e, down_e = gate_exps[0, 0], up_exps[0, 0], down_exps[0, 0]

    down_w = dense_matrix(down_values[0, 0], down_e, low_ids, width_blocks, hidden_blocks)
    gate_w = dense_matrix(gate_values[0, 0], gate_e, pair_ids, hidden_blocks, width_blocks)
    both = spread(jnp.concatenate([tokens, out_grad], axis=1), ("y", "core"))
    both, down_w, gate_w = lax.optimization_barrier((both, down_w, gate_w))
    place, place_z = lax.axis_index("x"), lax.axis_index("z")
    both = turn(both, -place)
    tokens_all, grads_all = both[:, :width], both[:, width:]

    swapped = swap_order(tokens_all, 4, 8)

    back_chunks = part_chunks(grads_all, down_w, False)
    gate_chunks = part_chunks(tokens_all, gate_w, True)
    up_w = dense_matrix(
        after(up_values, swapped, *gate_chunks)[0, 0], up_e, pair_ids, hidden_blocks, width_blocks
    )
    up_chunks = part_chunks(tokens_all, up_w, True)
    back_x, gate_x, up_x = cross_x(back_chunks), cross_x(gate_chunks), cross_x(up_chunks)
    back_sum = cross_z(after(back_x, *up_chunks), place_z)
    gate_sum = cross_z(gate_x, place_z)
    up_sum = cross_z(up_x, place_z)

    sigmoid = jax.nn.sigmoid(gate_sum)
    silu = gate_sum * sigmoid
    act = (silu * up_sum).astype(BF16)
    gate_piece = back_sum * up_sum * sigmoid * (1.0 + gate_sum * (1.0 - sigmoid))
    gate_piece, up_piece = gate_piece.astype(BF16), (back_sum * silu).astype(BF16)

    left = spread(jnp.concatenate([act, gate_piece, up_piece[:, :UP_CUT]], axis=1), "z")
    right = spread(jnp.concatenate(parts_x(up_piece[:, UP_CUT:]), axis=0), "z")
    act_parts = parts_x(left[:, :hidden])
    left_parts = parts_x(left[:, hidden:])

    output_part, down_grad = onward_and_grad(
        low_body, hidden_blocks, low_ids, down_e, grads_all, down_w, act_parts
    )
    output_rows = exchange_sum(turn(output_part, place), ("y", "core")).astype(BF16)
    input_part = swap_order(dot_nn(right, up_w[UP_CUT:], F32), 8, 4)
    left_parts = after(left_parts, down_grad, input_part)
    input_part = turned_sum(place, input_part, gate_w, up_w, left_parts)
    input_rows = exchange_sum(input_part, ("y", "core")).astype(BF16)
    gate_grad, up_grad = pair_grads(
        functools.partial(pair_body, width_blocks),
        (pair_ids, gate_e, up_e),
        (tokens_all, swapped, right, *left_parts),
        (hidden, width),
    )
    grads = (g[None, None] for g in (gate_grad, up_grad, down_grad))
    return output_rows, input_rows, *grads


def solution(mesh):
    shape = (4, 2, 4, 8)
    split = Mesh(mesh.devices.reshape(shape), ("y", "core", "x", "z"))
    row, col = ("y", "core"), ("x", "z")
    blocks, slots = P(row, col, None, None, None), P(row, col, None)
    return jax.shard_map(
        on_device,
        mesh=split,
        in_specs=(
            P(row, col),
            P(row, col),
            blocks,
            slots,
            blocks,
            slots,
            slots,
            blocks,
            slots,
            slots,
        ),
        out_specs=(P(row, col), P(row, col), blocks, blocks, blocks),
        check_vma=False,
    )
```

```python
import functools

import jax
import jax.numpy as jnp
from jax import lax
from jax.experimental import pallas as pl
from jax.experimental.pallas import tpu as pltpu
from jax.sharding import Mesh
from jax.sharding import PartitionSpec as P

FF_WIN = 28672
BLK = 128
F32, BF16 = jnp.float32, jnp.bfloat16
VMEM_LIMIT = 56 << 20
UP_CUT = 8 * BLK


def slot_scale(exponent):
    return jnp.where(exponent < 0, 0.5, jnp.where(exponent > 0, 2.0, 1.0)).astype(F32)


def place_body(in_blocks, block_count, ids, exps, values, dense):
    dense[...] = jnp.zeros_like(dense)

    def place(s, carry):
        block = ids[s]

        @pl.when(block < block_count)
        def _():
            row = pl.multiple_of(lax.div(block, in_blocks) * BLK, BLK)
            col = pl.multiple_of(lax.rem(block, in_blocks) * BLK, BLK)
            scaled = values[s].astype(F32) * slot_scale(exps[s])
            dense[pl.ds(row, BLK), pl.ds(col, BLK)] = scaled.astype(BF16)

        return carry

    lax.fori_loop(0, values.shape[0], place, 0)


def dense_matrix(values, exps, ids, out_blocks, in_blocks):
    return pl.pallas_call(
        functools.partial(place_body, in_blocks, out_blocks * in_blocks),
        out_shape=jax.ShapeDtypeStruct((out_blocks * BLK, in_blocks * BLK), BF16),
        in_specs=[
            pl.BlockSpec(memory_space=pltpu.SMEM),
            pl.BlockSpec(memory_space=pltpu.SMEM),
            pl.BlockSpec(memory_space=pltpu.VMEM),
        ],
        out_specs=pl.BlockSpec(memory_space=pltpu.VMEM),
        compiler_params=pltpu.CompilerParams(vmem_limit_bytes=VMEM_LIMIT),
    )(ids, exps, values)


def fill_dense(dense, column, out_acts, in_acts):
    wide = 2 * BLK
    for c in range(out_acts.shape[1] // wide):
        dense[column + c * wide : column + (c + 1) * wide, :] = lax.dot_general(
            out_acts[:, c * wide : (c + 1) * wide],
            in_acts[...],
            (((0,), (0,)), ((), ())),
            preferred_element_type=F32,
        )


def pick_slots(in_blocks, block_count, ids, exps, dense, grads):
    def pick(s, carry):
        block = ids[s]
        live = block < block_count

        @pl.when(live)
        def _():
            row = pl.multiple_of(lax.div(block, in_blocks) * BLK, BLK)
            col = pl.multiple_of(lax.rem(block, in_blocks) * BLK, BLK)
            picked = dense[pl.ds(row, BLK), pl.ds(col, BLK)] * slot_scale(exps[s])
            grads[s] = picked.astype(BF16)

        @pl.when(jnp.logical_not(live))
        def _():
            grads[s] = jnp.zeros((BLK, BLK), BF16)

        return carry

    lax.fori_loop(0, grads.shape[0], pick, 0)


def gather_parts(whole, parts):
    rows = whole.shape[0] // len(parts)
    for k, part in enumerate(parts):
        whole[k * rows : (k + 1) * rows, :] = part[...]


def pair_body(in_blocks, ids, gate_e, up_e, tokens, right_tokens, right, *rest):
    *parts, gate_g, up_g, left, dense = rest
    hidden = dense.shape[0]
    count = hidden // BLK * in_blocks
    gather_parts(left, parts)
    fill_dense(dense, 0, left.at[:, :hidden], tokens)
    pick_slots(in_blocks, count, ids, gate_e, dense, gate_g)
    fill_dense(dense, 0, left.at[:, hidden:], tokens)
    fill_dense(dense, left.shape[1] - hidden, right, right_tokens)
    pick_slots(in_blocks, count, ids, up_e, dense, up_g)


def pair_grads(body, scalars, arrays, dense_shape):
    slots = jax.ShapeDtypeStruct((scalars[0].shape[0], BLK, BLK), BF16)
    left = (arrays[0].shape[0], arrays[-1].shape[1])
    smem, vmem = (pl.BlockSpec(memory_space=m) for m in (pltpu.SMEM, pltpu.VMEM))
    return pl.pallas_call(
        body,
        out_shape=[slots] * 2,
        in_specs=[smem] * len(scalars) + [vmem] * len(arrays),
        out_specs=[vmem] * 2,
        scratch_shapes=[pltpu.VMEM(left, BF16), pltpu.VMEM(dense_shape, F32)],
        compiler_params=pltpu.CompilerParams(vmem_limit_bytes=VMEM_LIMIT),
    )(*scalars, *arrays)


def turned_body(place, first, gate_w, up_w, *rest):
    *parts, result, left = rest
    gather_parts(left, parts)
    cut = gate_w.shape[0]
    total = first[...] + jnp.dot(left[:, :cut], gate_w[...], preferred_element_type=F32)
    total = total + jnp.dot(
        left[:, cut:], up_w[...], preferred_element_type=F32
    )
    rows = total.shape[0] // 4
    for k in range(4):
        at = pl.multiple_of(lax.rem(place[0] + k, 4) * rows, rows)
        result[pl.ds(at, rows), :] = total[k * rows : (k + 1) * rows]


def turned_sum(place, first, gate_w, up_w, parts):
    rows, columns = len(parts) * parts[0].shape[0], parts[0].shape[1]
    smem = pl.BlockSpec(memory_space=pltpu.SMEM)

    def whole(array):
        return pl.BlockSpec(array.shape, lambda i: (0, 0))

    some_up = pl.BlockSpec((columns - gate_w.shape[0], up_w.shape[1]), lambda i: (0, 0))
    return pl.pallas_call(
        turned_body,
        grid=(1,),
        out_shape=jax.ShapeDtypeStruct(first.shape, F32),
        in_specs=[smem, whole(first), whole(gate_w), some_up] + [whole(part) for part in parts],
        out_specs=whole(first),
        scratch_shapes=[pltpu.VMEM((rows, columns), BF16)],
        compiler_params=pltpu.CompilerParams(vmem_limit_bytes=VMEM_LIMIT),
    )(place[None].astype(jnp.int32), first, gate_w, up_w, *parts)


def low_body(in_blocks, ids, exps, out_acts, matrix, *rest):
    *parts, onward, grads, whole, dense = rest
    gather_parts(whole, parts)
    onward[...] = lax.dot_general(
        whole[...], matrix[...], (((1,), (1,)), ((), ())), preferred_element_type=F32
    )
    flipped = out_acts[...].T
    wide = 2 * BLK
    for c in range(in_blocks * BLK // wide):
        cols = slice(c * wide, (c + 1) * wide)
        dense[:, cols] = jnp.dot(flipped, whole[:, cols], preferred_element_type=F32)
    pick_slots(in_blocks, dense.shape[0] // BLK * in_blocks, ids, exps, dense, grads)


def onward_and_grad(body, in_blocks, ids, exps, acts, matrix, parts):
    slots, columns = ids.shape[0], parts[0].shape[1]
    smem, vmem = (pl.BlockSpec(memory_space=m) for m in (pltpu.SMEM, pltpu.VMEM))
    onward, grads = pl.pallas_call(
        functools.partial(body, in_blocks),
        out_shape=[
            jax.ShapeDtypeStruct(acts.shape, F32),
            jax.ShapeDtypeStruct((slots, BLK, BLK), BF16),
        ],
        in_specs=[smem] * 2 + [vmem] * (2 + len(parts)),
        out_specs=[vmem] * 2,
        scratch_shapes=[
            pltpu.VMEM((acts.shape[0], columns), BF16),
            pltpu.VMEM(matrix.shape, F32),
        ],
        compiler_params=pltpu.CompilerParams(vmem_limit_bytes=VMEM_LIMIT),
    )(ids, exps, acts, matrix, *parts)
    return onward, grads


def part_body(flipped, acts, matrix, own, *sent):
    wide = 2 * BLK
    rows = own.shape[0]
    for c in range(own.shape[1] // wide):
        cols = slice(c * wide, (c + 1) * wide)
        if flipped:
            part = lax.dot_general(
                acts[...], matrix[cols, :], (((1,), (1,)), ((), ())), preferred_element_type=F32
            )
        else:
            part = jnp.dot(acts[...], matrix[:, cols], preferred_element_type=F32)
        own[:, cols] = part[:rows]
        for k, chunk in enumerate(sent):
            chunk[:, cols] = part[(k + 1) * rows : (k + 2) * rows].astype(BF16)


def part_chunks(acts, matrix, flipped):
    rows, columns = acts.shape[0] // 4, matrix.shape[0 if flipped else 1]
    vmem = pl.BlockSpec(memory_space=pltpu.VMEM)
    return pl.pallas_call(
        functools.partial(part_body, flipped),
        out_shape=[jax.ShapeDtypeStruct((rows, columns), F32)]
        + [jax.ShapeDtypeStruct((rows, columns), BF16)] * 3,
        in_specs=[vmem] * 2,
        out_specs=[vmem] * 4,
        compiler_params=pltpu.CompilerParams(vmem_limit_bytes=VMEM_LIMIT),
    )(acts, matrix)


def dot_nn(a, b, kind):
    return jnp.dot(a, b, preferred_element_type=F32).astype(kind)


def exchange_sum(part, axis):
    size = lax.axis_size(axis)
    got = lax.all_to_all(part, axis, split_axis=0, concat_axis=0, tiled=True)
    return jnp.sum(got.reshape(size, -1, part.shape[1]).astype(F32), axis=0)


def spread(rows, axis):
    size = lax.axis_size(axis)
    copies = jnp.broadcast_to(rows[None], (size, *rows.shape))
    copies = copies.reshape(size * rows.shape[0], rows.shape[1])
    return lax.all_to_all(copies, axis, split_axis=0, concat_axis=0, tiled=True)


def shift(rows, axis, step):
    size = lax.axis_size(axis)
    return lax.ppermute(rows, axis, [(i, (i + step) % size) for i in range(size)])


def turn(rows, steps):
    return jnp.roll(rows, steps * (rows.shape[0] // 4), axis=0)


def cross_x(chunks):
    total = chunks[0]
    for k in range(1, 4):
        total = total + shift(chunks[k], "x", k).astype(F32)
    return total


def own_rest(total, place_z):
    rows = total.shape[0] // 8
    own = lax.dynamic_slice_in_dim(total, place_z * rows, rows, axis=0)
    return own - lax.reduce_precision(own, exponent_bits=8, mantissa_bits=7)


def cross_z(total, place_z):
    return exchange_sum(total.astype(BF16), "z") + own_rest(total, place_z)


def swap_order(rows, outer, inner):
    grouped = rows.reshape(outer, inner, -1, rows.shape[1])
    return grouped.transpose(1, 0, 2, 3).reshape(rows.shape)


def after(value, *others):
    return lax.optimization_barrier((value, *others))[0]


def parts_x(rows):
    return [rows] + [shift(rows, "x", -k) for k in range(1, 4)]


def on_device(
    tokens,
    out_grad,
    gate_values,
    gate_exps,
    up_values,
    up_exps,
    gate_up_ids,
    down_values,
    down_exps,
    down_ids,
):
    width = tokens.shape[1]
    width_blocks = width // BLK
    hidden = FF_WIN // (lax.axis_size("y") * lax.axis_size("core"))
    hidden_blocks = hidden // BLK
    pair_ids, low_ids = gate_up_ids[0, 0], down_ids[0, 0]
    gate_e, up_e, down_e = gate_exps[0, 0], up_exps[0, 0], down_exps[0, 0]

    down_w = dense_matrix(down_values[0, 0], down_e, low_ids, width_blocks, hidden_blocks)
    gate_w = dense_matrix(gate_values[0, 0], gate_e, pair_ids, hidden_blocks, width_blocks)
    both = spread(jnp.concatenate([tokens, out_grad], axis=1), ("y", "core"))
    both, down_w, gate_w = lax.optimization_barrier((both, down_w, gate_w))
    place, place_z = lax.axis_index("x"), lax.axis_index("z")
    both = turn(both, -place)
    tokens_all, grads_all = both[:, :width], both[:, width:]

    swapped = swap_order(tokens_all, 4, 8)

    back_chunks = part_chunks(grads_all, down_w, False)
    gate_chunks = part_chunks(tokens_all, gate_w, True)
    up_w = dense_matrix(
        after(up_values, swapped, *gate_chunks)[0, 0], up_e, pair_ids, hidden_blocks, width_blocks
    )
    up_chunks = part_chunks(tokens_all, up_w, True)
    back_x, gate_x, up_x = cross_x(back_chunks), cross_x(gate_chunks), cross_x(up_chunks)
    back_sum = cross_z(after(back_x, *up_chunks), place_z)
    gate_sum = cross_z(gate_x, place_z)
    up_sum = cross_z(up_x, place_z)

    sigmoid = jax.nn.sigmoid(gate_sum)
    silu = gate_sum * sigmoid
    act = (silu * up_sum).astype(BF16)
    gate_piece = back_sum * up_sum * sigmoid * (1.0 + gate_sum * (1.0 - sigmoid))
    gate_piece, up_piece = gate_piece.astype(BF16), (back_sum * silu).astype(BF16)

    left = spread(jnp.concatenate([act, gate_piece, up_piece[:, :UP_CUT]], axis=1), "z")
    right = spread(jnp.concatenate(parts_x(up_piece[:, UP_CUT:]), axis=0), "z")
    act_parts = parts_x(left[:, :hidden])
    left_parts = parts_x(left[:, hidden:])

    output_part, down_grad = onward_and_grad(
        low_body, hidden_blocks, low_ids, down_e, grads_all, down_w, act_parts
    )
    output_rows = exchange_sum(turn(output_part, place), ("y", "core")).astype(BF16)
    input_part = swap_order(dot_nn(right, up_w[UP_CUT:], F32), 8, 4)
    left_parts = after(left_parts, down_grad, input_part)
    input_part = turned_sum(place, input_part, gate_w, up_w, left_parts)
    input_rows = exchange_sum(input_part, ("y", "core")).astype(BF16)
    gate_grad, up_grad = pair_grads(
        functools.partial(pair_body, width_blocks),
        (pair_ids, gate_e, up_e),
        (tokens_all, swapped, right, *left_parts),
        (hidden, width),
    )
    grads = (g[None, None] for g in (gate_grad, up_grad, down_grad))
    return output_rows, input_rows, *grads


def solution(mesh):
    shape = (4, 2, 4, 8)
    split = Mesh(mesh.devices.reshape(shape), ("y", "core", "x", "z"))
    row, col = ("y", "core"), ("x", "z")
    blocks, slots = P(row, col, None, None, None), P(row, col, None)
    return jax.shard_map(
        on_device,
        mesh=split,
        in_specs=(
            P(row, col),
            P(row, col),
            blocks,
            slots,
            blocks,
            slots,
            slots,
            blocks,
            slots,
            slots,
        ),
        out_specs=(P(row, col), P(row, col), blocks, blocks, blocks),
        check_vma=False,
    )
```
